1024 devices in a mesh: dp: 64 (over x_lo, z), expert: 16 (over x_hi, y, core).
Axes of the slice: x: 4 (x_hi: 2, x_lo: 2; x = x_hi * 2 + x_lo), y: 4, z: 32, core: 2. Of those that a mesh axis runs over, the one named last changes fastest.
Arguments:
- tokens: bfloat16 [32768, 3584], P('dp'), may hold values from -16 to 16
- grad_out: bfloat16 [32768, 3584], P('dp'), may hold values from -6 to 6
- route_rows: int32 [32768], P('dp'), may hold values from 0 to 511, as said below
- route_gate: float32 [32768], P('dp'), may hold values from 0.1 to 1
- block_count: int32 [64], P('dp'), may hold values from 0 to 4, as said below
- gate_weight: bfloat16 [3584, 2048], P('dp', 'expert'), may hold values from -0.25 to 0.25
- up_weight: bfloat16 [3584, 2048], P('dp', 'expert'), may hold values from -0.25 to 0.25
- down_weight_t: bfloat16 [3584, 2048], P('dp', 'expert'), may hold values from -0.125 to 0.125
Outputs:
- grad_tokens: bfloat16 [32768, 3584], P('dp', 'expert')
- grad_gate_weight: float32 [3584, 2048], P('dp', 'expert')
- grad_up_weight: float32 [3584, 2048], P('dp', 'expert')
The draws below stay inside these ranges and needn't reach their ends.
Inputs may be any that keep to these rules, and one draw needn't show every extreme that they name: `route_rows`: each index of dp holds 512 entries that are a permutation of 0 to 511. Slots 0 to block_count * 128 - 1 of an index of dp are live, its other slots empty; some index has all 4 blocks live and some index none.
All inputs are finite; a program needn't handle non-finite values.
Results may differ from the reference program's by a relative error of at most 0.017.
Values may be sent and summed in bfloat16 or wider, within the bound.
No kernel may reach another device: no remote copies, remote signals or barrier semaphores. Data moves between devices by JAX's collectives and lax.ppermute only.
A program may use at most 64 MiB of HBM per device.

```python
import math
import jax
import jax.numpy as jnp
from jax import lax

D = 3584
FF = 2048
T_DEV = 512
BLOCK = 128
NBLK = 4
HD = 128
TOKENS = 32768
N_DP = 64
N_EXPERT = 16


def draw_route_rows(key, part):
    device_keys = jax.random.split(jax.random.fold_in(key, 11), N_DP)
    orders = jax.vmap(lambda device_key: jax.random.permutation(device_key, T_DEV))(device_keys)
    return orders.reshape(-1).astype(jnp.int32)


def draw_block_count(key, part):
    levels = jax.random.randint(jax.random.fold_in(key, 21), (N_DP,), 0, 20)
    counts = jnp.where(levels < 4, 0, jnp.where(levels < 10, NBLK // 2, NBLK))
    chosen = jax.random.randint(jax.random.fold_in(key, 22), (), 0, N_DP)
    other_step = jax.random.randint(jax.random.fold_in(key, 23), (), 0, N_DP - 1)
    emptied = (chosen + 1 + other_step) % N_DP
    positions = jnp.arange(N_DP)
    counts = jnp.where(positions == chosen, NBLK, counts)
    counts = jnp.where(positions == emptied, 0, counts)
    return counts.astype(jnp.int32)


def strengthened(values, stream_key, source, target, blocks, factor):
    owner, partner = [(jnp.arange(values.shape[position]) // (values.shape[position] // blocks)).reshape([-1 if axis == position else 1 for axis in range(values.ndim)]) for position in (source, target)]
    chosen = jax.random.permutation(stream_key, blocks)[partner]
    strong = (owner == chosen) | (owner == (partner + blocks // 2) % blocks)
    return jnp.where(strong, factor * values, values)


def steps_of(own_key, dims, cuts, least, largest):
    def one(axis_at, shards_of):
        heights = jax.random.uniform(jax.random.fold_in(jax.random.fold_in(own_key, 6), axis_at), (shards_of,), jnp.float32, least / len(cuts), largest / len(cuts))
        return jnp.repeat(jnp.exp(heights), dims[axis_at] // shards_of).reshape((-1,) + (1,) * (len(dims) - axis_at - 1))

    level = one(*cuts[0])
    for cut in cuts[1:]:
        level = level * one(*cut)
    return level


def normal_values(own_key, shape, spread, reach, cuts=(), held_as=jnp.bfloat16):
    result = jax.random.normal(own_key, shape, jnp.float32) * spread
    if len(cuts) > 0:
        result = steps_of(own_key, shape, cuts, -0.22, 0.18) * result
    return jnp.clip(result, min=-reach, max=reach).astype(held_as)


def gaussian_with(stream_key, extent, deviation, limit, shards, heavy, dtype=jnp.bfloat16):
    result = deviation * jax.random.normal(stream_key, extent, jnp.float32)
    if shards:
        result = result * steps_of(stream_key, extent, shards, -0.22, 0.18)
    return jnp.clip(strengthened(result, jax.random.fold_in(stream_key, 3), *heavy), -limit, limit).astype(dtype)


def setup_inputs(seed: int = 0) -> dict:
    splits = jax.random.split(jax.random.key(seed), 9)
    tokens = gaussian_with(splits[0], (TOKENS, D), 1.0, 16.0, ((0, 64),), (0, 1, 64, 4.0))
    grad_out = normal_values(splits[1], (TOKENS, D), 1.0, 6.0, ((0, 64),))
    route_rows = draw_route_rows(jax.random.fold_in(splits[8], 71), 0)
    route_gate = jnp.clip(jnp.exp(math.log(1.0) - 2.3025851 * jax.random.uniform(splits[3], (TOKENS,), jnp.float32) ** steps_of(splits[3], (TOKENS,), ((0, 64),), -0.2, 0.2)), 0.1, 1.0)
    block_count = draw_block_count(jax.random.fold_in(splits[8], 71), 0)
    gate_weight = gaussian_with(splits[5], (D, FF), D ** -0.5, 0.25, ((0, 64), (1, 16)), (1, 0, 64, 4.0))
    up_weight = gaussian_with(splits[6], (D, FF), D ** -0.5, 0.25, ((0, 64), (1, 16)), (1, 0, 64, 4.0))
    down_weight_t = normal_values(splits[7], (D, FF), FF ** -0.5, 0.125, ((0, 64), (1, 16)))
    return {"tokens": tokens, "grad_out": grad_out, "route_rows": route_rows, "route_gate": route_gate, "block_count": block_count, "gate_weight": gate_weight, "up_weight": up_weight, "down_weight_t": down_weight_t}


def reference(tokens, grad_out, route_rows, route_gate, block_count, gate_weight, up_weight, down_weight_t):
    def device_pass(running, device_item):
        sum_gate, sum_up = running
        token_dev, cotangent_dev, rows_dev, gates_dev, live_count = device_item

        def block_step(block_index, state_inner):
            acc_gate, acc_up, input_dev = state_inner
            offset = block_index * BLOCK
            rows_block = lax.dynamic_slice_in_dim(rows_dev, offset, BLOCK, 0)
            token_block = jnp.take(token_dev, rows_block, axis=0)
            cotangent_block = jnp.take(cotangent_dev, rows_block, axis=0)
            weight_block = lax.dynamic_slice_in_dim(gates_dev, offset, BLOCK, 0)
            gate_val = jnp.dot(token_block, gate_weight, preferred_element_type=jnp.float32)
            up_val = jnp.dot(token_block, up_weight, preferred_element_type=jnp.float32)
            backward = jnp.dot(cotangent_block, down_weight_t, preferred_element_type=jnp.float32)
            hidden_grad = weight_block[:, None] * backward
            gate_sigmoid = jax.nn.sigmoid(gate_val)
            grad_up = (hidden_grad * (gate_val * gate_sigmoid)).astype(jnp.bfloat16)
            grad_gate = (hidden_grad * up_val * gate_sigmoid * (1.0 + gate_val * (1.0 - gate_sigmoid))).astype(jnp.bfloat16)
            summed_rows = jnp.zeros((BLOCK, D), jnp.float32)
            for column_group in range(N_EXPERT):
                lower_col = column_group * HD
                upper_col = lower_col + HD
                partial_sum = jnp.dot(grad_gate[:, lower_col:upper_col], gate_weight[:, lower_col:upper_col].T, preferred_element_type=jnp.float32)
                partial_sum = partial_sum + jnp.dot(grad_up[:, lower_col:upper_col], up_weight[:, lower_col:upper_col].T, preferred_element_type=jnp.float32)
                partial_sum = lax.optimization_barrier(partial_sum.astype(jnp.bfloat16))
                summed_rows = summed_rows + partial_sum.astype(jnp.float32)
            input_dev = input_dev.at[rows_block].set(summed_rows.astype(jnp.bfloat16))
            acc_gate = acc_gate + jnp.dot(token_block.T, grad_gate, preferred_element_type=jnp.float32)
            acc_up = acc_up + jnp.dot(token_block.T, grad_up, preferred_element_type=jnp.float32)
            return acc_gate, acc_up, input_dev

        start_state = (sum_gate, sum_up, jnp.zeros((T_DEV, D), jnp.bfloat16))
        sum_gate, sum_up, input_dev = lax.fori_loop(0, live_count, block_step, start_state)
        return (sum_gate, sum_up), input_dev

    zero_grad = jnp.zeros((D, FF), jnp.float32)
    device_items = (tokens.reshape(N_DP, T_DEV, D), grad_out.reshape(N_DP, T_DEV, D), route_rows.reshape(N_DP, T_DEV), route_gate.reshape(N_DP, T_DEV), block_count)
    (sum_gate, sum_up), inputs_all = lax.scan(device_pass, (zero_grad, zero_grad), device_items)
    grad_scale = float(TOKENS) ** -0.5
    return inputs_all.reshape(TOKENS, D), sum_gate * grad_scale, sum_up * grad_scale
```

```python
import jax
import jax.numpy as jnp
from jax import lax
from jax.sharding import Mesh, PartitionSpec as P

BLOCK = 128
SIZES = {"side": 2, "far": 16, "near": 2, "wide": 2, "ring": 4, "core": 2}
SIDE, FAR, NEAR, WIDE, RING, CORE = SIZES.values()
DP = ("side", "far", "near")
QUAD = ("side", "near")
EXPERT = ("wide", "ring", "core")

ROWS_CONTRACT = (((0,), (0,)), ((), ()))
COLS_CONTRACT = (((1,), (1,)), ((), ()))


def summed(terms):
    total = terms[0].astype(jnp.float32)
    for term in terms[1:]:
        total = total + term.astype(jnp.float32)
    return total


def shifted_term(parts, axis, dim, shift):
    count = SIZES[axis]
    index = lax.axis_index(axis)
    sent = lax.dynamic_index_in_dim(parts, (index + shift) % count, dim, keepdims=False)
    if shift == 0:
        return sent
    return lax.ppermute(sent, axis, [(i, (i + shift) % count) for i in range(count)])


def permuted_sum(parts, axis, dim):
    shifts = [0, 1, SIZES[axis] - 1] + list(range(2, SIZES[axis] - 1))
    shifts = shifts[: SIZES[axis]]
    return summed([shifted_term(parts, axis, dim, shift) for shift in shifts])


def exchanged_sum(parts, axes):
    terms = lax.all_to_all(parts, axes, 0, 0, tiled=True)
    return summed([terms[i] for i in range(terms.shape[0])])


def local(
    tokens, grad_out, route_rows, route_gate, block_count, gate_weight, up_weight, down_weight_t
):
    own_rows, hidden_width = gate_weight.shape
    slot_count = route_rows.shape[0]
    feature_count = tokens.shape[1]

    slots = jnp.arange(slot_count, dtype=jnp.int32)
    slot_gate = jnp.where(slots // BLOCK < block_count[0], route_gate, 0.0)
    carried = route_rows[:, None] == slots[None, :]
    token_gate = jnp.sum(jnp.where(carried, slot_gate[:, None], 0.0), axis=0)

    owned = jnp.concatenate([gate_weight, up_weight, down_weight_t], axis=1)
    far_rows = lax.all_gather(owned, "far", axis=0, tiled=True)
    quads = jnp.broadcast_to(far_rows[None], (SIDE * NEAR, *far_rows.shape))
    quads = lax.all_to_all(quads, QUAD, 0, 0, tiled=True)
    panels = quads.reshape(SIDE, NEAR, FAR, own_rows, 3 * hidden_width)
    panels = panels.swapaxes(1, 2).reshape(feature_count, 3 * hidden_width)
    both_panels = panels[:, : 2 * hidden_width]
    down_panel = panels[:, 2 * hidden_width :]

    projected = jnp.dot(tokens, both_panels, preferred_element_type=jnp.float32)
    back = jnp.dot(grad_out, down_panel, preferred_element_type=jnp.float32)
    gate_val = projected[:, :hidden_width]
    up_val = projected[:, hidden_width:]
    hidden_grad = token_gate[:, None] * back
    gate_sigmoid = jax.nn.sigmoid(gate_val)
    grad_up = hidden_grad * (gate_val * gate_sigmoid)
    grad_gate = hidden_grad * up_val * gate_sigmoid * (1.0 + gate_val * (1.0 - gate_sigmoid))
    grads = jnp.concatenate([grad_gate, grad_up], axis=1).astype(jnp.bfloat16)

    weight_terms = lax.dot_general(
        tokens, grads, ROWS_CONTRACT, preferred_element_type=jnp.float32
    ).astype(jnp.bfloat16)
    by_quad = weight_terms.reshape(SIDE, FAR, NEAR, own_rows, 2 * hidden_width)
    by_quad = by_quad.swapaxes(1, 2).reshape(SIDE * NEAR, FAR, own_rows, 2 * hidden_width)
    quad_sum = exchanged_sum(by_quad, QUAD).astype(jnp.bfloat16)
    weight_share = exchanged_sum(quad_sum, "far")
    grad_scale = float(SIDE * FAR * NEAR * slot_count) ** (-0.5)
    weight_share = weight_share * grad_scale

    input_terms = lax.dot_general(
        both_panels, grads, COLS_CONTRACT, preferred_element_type=jnp.float32
    ).astype(jnp.bfloat16)
    own_features = feature_count // (WIDE * RING * CORE)
    by_expert = input_terms.reshape(WIDE, RING, CORE, own_features, slot_count)
    core_sum = permuted_sum(by_expert, "core", 2).astype(jnp.bfloat16)
    ring_sum = permuted_sum(core_sum, "ring", 1).astype(jnp.bfloat16)
    wide_sum = permuted_sum(ring_sum, "wide", 0).astype(jnp.bfloat16)
    grad_tokens = wide_sum.T
    return grad_tokens, weight_share[:, :hidden_width], weight_share[:, hidden_width:]


def solution(mesh):
    fine_mesh = Mesh(mesh.devices.reshape(tuple(SIZES.values())), tuple(SIZES))
    in_specs = (P(DP, None), P(DP, None), P(DP), P(DP), P(DP)) + (P(DP, EXPERT),) * 3
    out_specs = (P(DP, EXPERT),) * 3
    return jax.shard_map(
        local, mesh=fine_mesh, in_specs=in_specs, out_specs=out_specs, check_vma=False
    )
```

```python
import jax
import jax.numpy as jnp
from jax import lax
from jax.sharding import Mesh, PartitionSpec as P

BLOCK = 128
SIZES = {"side": 2, "far": 16, "near": 2, "wide": 2, "ring": 4, "core": 2}
SIDE, FAR, NEAR, WIDE, RING, CORE = SIZES.values()
DP = ("side", "far", "near")
QUAD = ("side", "near")
EXPERT = ("wide", "ring", "core")

ROWS_CONTRACT = (((0,), (0,)), ((), ()))
COLS_CONTRACT = (((1,), (1,)), ((), ()))


def summed(terms):
    total = terms[0].astype(jnp.float32)
    for term in terms[1:]:
        total = total + term.astype(jnp.float32)
    return total


def shifted_term(parts, axis, dim, shift):
    count = SIZES[axis]
    index = lax.axis_index(axis)
    sent = lax.dynamic_index_in_dim(parts, (index + shift) % count, dim, keepdims=False)
    if shift == 0:
        return sent
    return lax.ppermute(sent, axis, [(i, (i + shift) % count) for i in range(count)])


def permuted_sum(parts, axis, dim):
    shifts = [0, 1, SIZES[axis] - 1] + list(range(2, SIZES[axis] - 1))
    shifts = shifts[: SIZES[axis]]
    return summed([shifted_term(parts, axis, dim, shift) for shift in shifts])


def exchanged_sum(parts, axes):
    terms = lax.all_to_all(parts, axes, 0, 0, tiled=True)
    return summed([terms[i] for i in range(terms.shape[0])])


def local(
    tokens, grad_out, route_rows, route_gate, block_count, gate_weight, up_weight, down_weight_t
):
    own_rows, hidden_width = gate_weight.shape
    slot_count = route_rows.shape[0]
    feature_count = tokens.shape[1]

    slots = jnp.arange(slot_count, dtype=jnp.int32)
    slot_gate = jnp.where(slots // BLOCK < block_count[0], route_gate, 0.0)
    carried = route_rows[:, None] == slots[None, :]
    token_gate = jnp.sum(jnp.where(carried, slot_gate[:, None], 0.0), axis=0)

    owned = jnp.concatenate([gate_weight, up_weight, down_weight_t], axis=1)
    far_rows = lax.all_gather(owned, "far", axis=0, tiled=True)
    far_rows, early_tokens = lax.optimization_barrier((far_rows, tokens))
    feature_rows = early_tokens.T.reshape(SIDE, FAR, NEAR, own_rows, slot_count)
    feature_rows = lax.optimization_barrier(feature_rows.swapaxes(1, 2))
    quads = jnp.broadcast_to(far_rows[None], (SIDE * NEAR, *far_rows.shape))
    quads = lax.all_to_all(quads, QUAD, 0, 0, tiled=True)
    panels = quads.reshape(SIDE, NEAR, FAR, own_rows, 3 * hidden_width)
    panels = panels.swapaxes(1, 2).reshape(feature_count, 3 * hidden_width)
    both_panels = panels[:, : 2 * hidden_width]
    down_panel = panels[:, 2 * hidden_width :]

    projected = jnp.dot(tokens, both_panels, preferred_element_type=jnp.float32)
    back = jnp.dot(grad_out, down_panel, preferred_element_type=jnp.float32)
    gate_val = projected[:, :hidden_width]
    up_val = projected[:, hidden_width:]
    hidden_grad = token_gate[:, None] * back
    gate_sigmoid = jax.nn.sigmoid(gate_val)
    grad_up = hidden_grad * (gate_val * gate_sigmoid)
    grad_gate = hidden_grad * up_val * gate_sigmoid * (1.0 + gate_val * (1.0 - gate_sigmoid))
    grads = jnp.concatenate([grad_gate, grad_up], axis=1).astype(jnp.bfloat16)

    weight_terms = jnp.dot(
        feature_rows.reshape(feature_count, slot_count), grads, preferred_element_type=jnp.float32
    ).astype(jnp.bfloat16)
    by_quad = weight_terms.reshape(SIDE * NEAR, FAR, own_rows, 2 * hidden_width)
    quad_terms = lax.all_to_all(by_quad, QUAD, 0, 0, tiled=True)

    input_terms = lax.dot_general(
        both_panels, grads, COLS_CONTRACT, preferred_element_type=jnp.float32
    ).astype(jnp.bfloat16)
    own_features = feature_count // (WIDE * RING * CORE)
    by_expert = input_terms.reshape(WIDE, RING, CORE, own_features, slot_count)
    core_sum = permuted_sum(by_expert, "core", 2).astype(jnp.bfloat16)
    quad_terms, _ = lax.optimization_barrier((quad_terms, core_sum))
    quad_sum = summed([quad_terms[i] for i in range(SIDE * NEAR)]).astype(jnp.bfloat16)
    weight_share = exchanged_sum(quad_sum, "far")
    grad_scale = float(SIDE * FAR * NEAR * slot_count) ** (-0.5)
    weight_share = weight_share * grad_scale
    ring_sum = permuted_sum(core_sum, "ring", 1).astype(jnp.bfloat16)
    wide_sum = permuted_sum(ring_sum, "wide", 0).astype(jnp.bfloat16)
    grad_tokens = wide_sum.T
    return grad_tokens, weight_share[:, :hidden_width], weight_share[:, hidden_width:]


def solution(mesh):
    fine_mesh = Mesh(mesh.devices.reshape(tuple(SIZES.values())), tuple(SIZES))
    in_specs = (P(DP, None), P(DP, None), P(DP), P(DP), P(DP)) + (P(DP, EXPERT),) * 3
    out_specs = (P(DP, EXPERT),) * 3
    return jax.shard_map(
        local, mesh=fine_mesh, in_specs=in_specs, out_specs=out_specs, check_vma=False
    )
```

```python
import jax
import jax.numpy as jnp
from jax import lax
from jax.experimental.layout import Layout, with_layout_constraint
from jax.sharding import Mesh, PartitionSpec as P

BLOCK = 128
SIZES = {"side": 2, "far": 8, "mid": 2, "near": 2, "wide": 2, "ring": 4, "core": 2}
SIDE, FAR, MID, NEAR, WIDE, RING, CORE = SIZES.values()
DP = ("side", "far", "mid", "near")
SECONDS = ("far", "mid")
QUAD = ("side", "near")
NEIGHBOURS = ("mid", "near")
SWAP = [(0, 1), (1, 0)]
EXPERT = ("wide", "ring", "core")

ROWS_CONTRACT = (((0,), (0,)), ((), ()))
COLS_CONTRACT = (((1,), (1,)), ((), ()))


def row_major(array):
    return with_layout_constraint(array, Layout(major_to_minor=(0, 1)))


def summed(terms):
    total = terms[0].astype(jnp.float32)
    for term in terms[1:]:
        total = total + term.astype(jnp.float32)
    return total


def shifted_term(parts, axis, dim, shift):
    count = SIZES[axis]
    index = lax.axis_index(axis)
    sent = lax.dynamic_index_in_dim(parts, (index + shift) % count, dim, keepdims=False)
    if shift == 0:
        return sent
    return lax.ppermute(sent, axis, [(i, (i + shift) % count) for i in range(count)])


def permuted_sum(parts, axis, dim):
    shifts = [0, 1, SIZES[axis] - 1] + list(range(2, SIZES[axis] - 1))
    shifts = shifts[: SIZES[axis]]
    return summed([shifted_term(parts, axis, dim, shift) for shift in shifts])


def exchanged_sum(parts, axes):
    terms = lax.all_to_all(parts, axes, 0, 0, tiled=True)
    return summed([terms[i] for i in range(terms.shape[0])])


def local(
    tokens, grad_out, route_rows, route_gate, block_count, gate_weight, up_weight, down_weight_t
):
    own_rows, hidden_width = gate_weight.shape
    slot_count = route_rows.shape[0]
    feature_count = tokens.shape[1]

    slots = jnp.arange(slot_count, dtype=jnp.int32)
    slot_gate = jnp.where(slots // BLOCK < block_count[0], route_gate, 0.0)
    carried = route_rows[:, None] == slots[None, :]
    token_gate = jnp.sum(jnp.where(carried, slot_gate[:, None], 0.0), axis=0)

    side_index = lax.axis_index("side")
    core_index = lax.axis_index("core")
    half_features = feature_count // SIDE
    half_slots = slot_count // CORE
    sent_tokens = lax.dynamic_slice(
        tokens,
        (core_index * half_slots, (1 - side_index) * half_features),
        (half_slots, half_features),
    )
    fetched_tokens = row_major(lax.ppermute(row_major(sent_tokens), "side", SWAP))

    owned = jnp.concatenate([gate_weight, up_weight, down_weight_t], axis=1)
    far_rows = lax.all_gather(owned, SECONDS, axis=0, tiled=True)
    far_rows, fetched_tokens, early_tokens = lax.optimization_barrier(
        (far_rows, fetched_tokens, tokens)
    )
    swapped_tokens = row_major(lax.ppermute(fetched_tokens, "core", SWAP))
    kept_tokens = lax.dynamic_slice_in_dim(early_tokens, side_index * half_features, half_features, 1)
    feature_rows = jnp.concatenate([kept_tokens, fetched_tokens, swapped_tokens], axis=0).T
    feature_rows = feature_rows.reshape(FAR, MID * NEAR, own_rows, SIDE * slot_count)
    feature_rows = lax.optimization_barrier(feature_rows.swapaxes(0, 1))
    quads = jnp.broadcast_to(far_rows[None], (SIDE * NEAR, *far_rows.shape))
    quads = lax.all_to_all(quads, QUAD, 0, 0, tiled=True)
    quads, feature_rows = lax.optimization_barrier((quads, feature_rows))
    panels = quads.reshape(SIDE, NEAR, FAR * MID, own_rows, 3 * hidden_width)
    panels = panels.swapaxes(1, 2).reshape(feature_count, 3 * hidden_width)
    both_panels = panels[:, : 2 * hidden_width]
    down_panel = panels[:, 2 * hidden_width :]

    projected = jnp.dot(tokens, both_panels, preferred_element_type=jnp.float32)
    back = jnp.dot(grad_out, down_panel, preferred_element_type=jnp.float32)
    gate_val = projected[:, :hidden_width]
    up_val = projected[:, hidden_width:]
    hidden_grad = token_gate[:, None] * back
    gate_sigmoid = jax.nn.sigmoid(gate_val)
    grad_up = hidden_grad * (gate_val * gate_sigmoid)
    grad_gate = hidden_grad * up_val * gate_sigmoid * (1.0 + gate_val * (1.0 - gate_sigmoid))
    grads = jnp.concatenate([grad_gate, grad_up], axis=1).astype(jnp.bfloat16)

    turned = jnp.concatenate([grads[half_slots:], grads[:half_slots]], axis=0)
    sent_grads = jnp.where(core_index == 0, grads, turned)
    both_grads = jnp.concatenate([grads, lax.ppermute(sent_grads, "side", SWAP)], axis=0)
    weight_terms = jnp.dot(
        feature_rows.reshape(half_features, SIDE * slot_count),
        both_grads,
        preferred_element_type=jnp.float32,
    ).astype(jnp.bfloat16)
    weight_terms = weight_terms.reshape(MID * NEAR, FAR, own_rows, 2 * hidden_width)
    near_terms = lax.all_to_all(weight_terms, NEIGHBOURS, 0, 0, tiled=True)

    input_terms = lax.dot_general(
        both_panels, grads, COLS_CONTRACT, preferred_element_type=jnp.float32
    ).astype(jnp.bfloat16)
    own_features = feature_count // (WIDE * RING * CORE)
    by_expert = input_terms.reshape(WIDE, RING, CORE, own_features, slot_count)
    core_sum = permuted_sum(by_expert, "core", 2).astype(jnp.bfloat16)
    near_terms, _ = lax.optimization_barrier((near_terms, core_sum))
    near_sum = summed([near_terms[i] for i in range(MID * NEAR)]).astype(jnp.bfloat16)
    weight_share = exchanged_sum(near_sum, "far")
    grad_scale = float(SIDE * FAR * MID * NEAR * slot_count) ** (-0.5)
    weight_share = weight_share * grad_scale
    ring_sum = permuted_sum(core_sum, "ring", 1).astype(jnp.bfloat16)
    wide_sum = permuted_sum(ring_sum, "wide", 0).astype(jnp.bfloat16)
    grad_tokens = wide_sum.T
    return grad_tokens, weight_share[:, :hidden_width], weight_share[:, hidden_width:]


def solution(mesh):
    fine_mesh = Mesh(mesh.devices.reshape(tuple(SIZES.values())), tuple(SIZES))
    in_specs = (P(DP, None), P(DP, None), P(DP), P(DP), P(DP)) + (P(DP, EXPERT),) * 3
    out_specs = (P(DP, EXPERT),) * 3
    return jax.shard_map(
        local, mesh=fine_mesh, in_specs=in_specs, out_specs=out_specs, check_vma=False
    )
```

```python
import jax
import jax.numpy as jnp
from jax import lax
from jax.experimental.layout import Layout, with_layout_constraint
from jax.sharding import Mesh, PartitionSpec as P

BLOCK = 128
SIZES = {"side": 2, "far": 8, "mid": 2, "near": 2, "wide": 2, "ring": 4, "core": 2}
SIDE, FAR, MID, NEAR, WIDE, RING, CORE = SIZES.values()
DP = ("side", "far", "mid", "near")
SECONDS = ("far", "mid")
QUAD = ("side", "near")
NEIGHBOURS = ("mid", "near")
SWAP = [(0, 1), (1, 0)]
EXPERT = ("wide", "ring", "core")

ROWS_CONTRACT = (((0,), (0,)), ((), ()))
COLS_CONTRACT = (((1,), (1,)), ((), ()))


def row_major(array):
    return with_layout_constraint(array, Layout(major_to_minor=(0, 1)))


def summed(terms):
    total = terms[0].astype(jnp.float32)
    for term in terms[1:]:
        total = total + term.astype(jnp.float32)
    return total


def part_for(parts, axis, dim, shift):
    index = (lax.axis_index(axis) + shift) % SIZES[axis]
    return lax.dynamic_index_in_dim(parts, index, dim, keepdims=False)


def moved(part, axis, shift):
    return lax.ppermute(part, axis, [(i, (i + shift) % SIZES[axis]) for i in range(SIZES[axis])])


def exchanged_sum(parts, axes):
    terms = lax.all_to_all(parts, axes, 0, 0, tiled=True)
    return summed([terms[i] for i in range(terms.shape[0])])


def local(
    tokens, grad_out, route_rows, route_gate, block_count, gate_weight, up_weight, down_weight_t
):
    own_rows, hidden_width = gate_weight.shape
    slot_count = route_rows.shape[0]
    feature_count = tokens.shape[1]

    slots = jnp.arange(slot_count, dtype=jnp.int32)
    slot_gate = jnp.where(slots // BLOCK < block_count[0], route_gate, 0.0)
    carried = route_rows[:, None] == slots[None, :]
    token_gate = jnp.sum(jnp.where(carried, slot_gate[:, None], 0.0), axis=0)

    side_index = lax.axis_index("side")
    core_index = lax.axis_index("core")
    half_features = feature_count // SIDE
    half_slots = slot_count // CORE
    sent_tokens = lax.dynamic_slice(
        tokens,
        (core_index * half_slots, (1 - side_index) * half_features),
        (half_slots, half_features),
    )
    fetched_tokens = row_major(lax.ppermute(row_major(sent_tokens), "side", SWAP))

    owned = jnp.concatenate([gate_weight, up_weight, down_weight_t], axis=1)
    far_rows = lax.all_gather(owned, SECONDS, axis=0, tiled=True)
    far_rows, fetched_tokens, early_tokens = lax.optimization_barrier(
        (far_rows, fetched_tokens, tokens)
    )
    swapped_tokens = row_major(lax.ppermute(fetched_tokens, "core", SWAP))
    kept_tokens = lax.dynamic_slice_in_dim(early_tokens, side_index * half_features, half_features, 1)
    feature_rows = jnp.concatenate([kept_tokens, fetched_tokens, swapped_tokens], axis=0).T
    feature_rows = feature_rows.reshape(FAR, MID * NEAR, own_rows, SIDE * slot_count)
    feature_rows = lax.optimization_barrier(feature_rows.swapaxes(0, 1))
    quads = jnp.broadcast_to(far_rows[None], (SIDE * NEAR, *far_rows.shape))
    quads = lax.all_to_all(quads, QUAD, 0, 0, tiled=True)
    quads, feature_rows = lax.optimization_barrier((quads, feature_rows))
    panels = quads.reshape(SIDE, NEAR, FAR * MID, own_rows, 3 * hidden_width)
    panels = panels.swapaxes(1, 2).reshape(feature_count, 3 * hidden_width)
    both_panels = panels[:, : 2 * hidden_width]
    down_panel = panels[:, 2 * hidden_width :]

    projected = jnp.dot(tokens, both_panels, preferred_element_type=jnp.float32)
    back = jnp.dot(grad_out, down_panel, preferred_element_type=jnp.float32)
    gate_val = projected[:, :hidden_width]
    up_val = projected[:, hidden_width:]
    hidden_grad = token_gate[:, None] * back
    gate_sigmoid = jax.nn.sigmoid(gate_val)
    grad_up = hidden_grad * (gate_val * gate_sigmoid)
    grad_gate = hidden_grad * up_val * gate_sigmoid * (1.0 + gate_val * (1.0 - gate_sigmoid))
    grads = jnp.concatenate([grad_gate, grad_up], axis=1).astype(jnp.bfloat16)

    turned = jnp.concatenate([grads[half_slots:], grads[:half_slots]], axis=0)
    sent_grads = jnp.where(core_index == 0, grads, turned)
    partner_grads = lax.ppermute(sent_grads, "side", SWAP)

    input_terms = lax.dot_general(
        both_panels, grads, COLS_CONTRACT, preferred_element_type=jnp.float32
    ).astype(jnp.bfloat16)
    own_features = feature_count // (WIDE * RING * CORE)
    by_expert = input_terms.reshape(WIDE, RING, CORE, own_features, slot_count)
    core_sent = part_for(by_expert, "core", 2, 1)
    core_terms = [part_for(by_expert, "core", 2, 0), moved(core_sent, "core", 1)]

    partner_grads, _ = lax.optimization_barrier((partner_grads, core_sent))
    both_grads = jnp.concatenate([grads, partner_grads], axis=0)
    weight_terms = jnp.dot(
        feature_rows.reshape(half_features, SIDE * slot_count),
        both_grads,
        preferred_element_type=jnp.float32,
    ).astype(jnp.bfloat16)
    weight_terms = weight_terms.reshape(MID * NEAR, FAR, own_rows, 2 * hidden_width)
    near_terms = lax.all_to_all(weight_terms, NEIGHBOURS, 0, 0, tiled=True)

    core_sum = summed(core_terms).astype(jnp.bfloat16)
    ring_terms = [part_for(core_sum, "ring", 1, 0)]
    for shift in (1, RING - 1, 2):
        ring_terms.append(moved(part_for(core_sum, "ring", 1, shift), "ring", shift))
    near_terms, ring_terms = lax.optimization_barrier((near_terms, ring_terms))
    near_sum = summed([near_terms[i] for i in range(MID * NEAR)]).astype(jnp.bfloat16)
    weight_share = exchanged_sum(near_sum, "far")

    ring_sum = summed(ring_terms).astype(jnp.bfloat16)
    wide_terms = [part_for(ring_sum, "wide", 0, 0), moved(part_for(ring_sum, "wide", 0, 1), "wide", 1)]
    grad_tokens = summed(wide_terms).astype(jnp.bfloat16).T
    grad_scale = float(SIDE * FAR * MID * NEAR * slot_count) ** (-0.5)
    weight_share = weight_share * grad_scale
    return grad_tokens, weight_share[:, :hidden_width], weight_share[:, hidden_width:]


def solution(mesh):
    fine_mesh = Mesh(mesh.devices.reshape(tuple(SIZES.values())), tuple(SIZES))
    in_specs = (P(DP, None), P(DP, None), P(DP), P(DP), P(DP)) + (P(DP, EXPERT),) * 3
    out_specs = (P(DP, EXPERT),) * 3
    return jax.shard_map(
        local, mesh=fine_mesh, in_specs=in_specs, out_specs=out_specs, check_vma=False
    )
```

```python
import jax
import jax.numpy as jnp
from jax import lax
from jax.experimental.layout import Layout, with_layout_constraint
from jax.sharding import Mesh, PartitionSpec as P

BLOCK = 128
SIZES = {"side": 2, "far": 8, "mid": 2, "near": 2, "wide": 2, "ring": 4, "core": 2}
SIDE, FAR, MID, NEAR, WIDE, RING, CORE = SIZES.values()
DP = ("side", "far", "mid", "near")
SECONDS = ("far", "mid")
QUAD = ("side", "near")
NEIGHBOURS = ("mid", "near")
SWAP = [(0, 1), (1, 0)]
EXPERT = ("wide", "ring", "core")

ROWS_CONTRACT = (((0,), (0,)), ((), ()))
COLS_CONTRACT = (((1,), (1,)), ((), ()))


def row_major(array):
    return with_layout_constraint(array, Layout(major_to_minor=(0, 1)))


def summed(terms):
    total = terms[0].astype(jnp.float32)
    for term in terms[1:]:
        total = total + term.astype(jnp.float32)
    return total


def part_for(parts, axis, dim, shift):
    index = (lax.axis_index(axis) + shift) % SIZES[axis]
    return lax.dynamic_index_in_dim(parts, index, dim, keepdims=False)


def moved(part, axis, shift):
    return lax.ppermute(part, axis, [(i, (i + shift) % SIZES[axis]) for i in range(SIZES[axis])])


def exchanged_sum(parts, axes):
    terms = lax.all_to_all(parts, axes, 0, 0, tiled=True)
    return summed([terms[i] for i in range(terms.shape[0])])


def local(
    tokens, grad_out, route_rows, route_gate, block_count, gate_weight, up_weight, down_weight_t
):
    own_rows, hidden_width = gate_weight.shape
    slot_count = route_rows.shape[0]
    feature_count = tokens.shape[1]

    slots = jnp.arange(slot_count, dtype=jnp.int32)
    slot_gate = jnp.where(slots // BLOCK < block_count[0], route_gate, 0.0)
    carried = route_rows[:, None] == slots[None, :]
    token_gate = jnp.sum(jnp.where(carried, slot_gate[:, None], 0.0), axis=0)

    side_index = lax.axis_index("side")
    core_index = lax.axis_index("core")
    half_features = feature_count // SIDE
    half_slots = slot_count // CORE
    sent_tokens = lax.dynamic_slice(
        tokens,
        (core_index * half_slots, (1 - side_index) * half_features),
        (half_slots, half_features),
    )
    fetched_tokens = row_major(lax.ppermute(row_major(sent_tokens), "side", SWAP))

    owned = jnp.concatenate([gate_weight, up_weight, down_weight_t], axis=1)
    far_rows = lax.all_gather(owned, SECONDS, axis=0, tiled=True)
    far_rows, fetched_tokens, early_tokens = lax.optimization_barrier(
        (far_rows, fetched_tokens, tokens)
    )
    swapped_tokens = row_major(lax.ppermute(fetched_tokens, "core", SWAP))
    kept_tokens = lax.dynamic_slice_in_dim(early_tokens, side_index * half_features, half_features, 1)
    feature_rows = jnp.concatenate([kept_tokens, fetched_tokens, swapped_tokens], axis=0).T
    feature_rows = feature_rows.reshape(FAR, MID * NEAR, own_rows, SIDE * slot_count)
    feature_rows = lax.optimization_barrier(feature_rows.swapaxes(0, 1))
    quads = jnp.broadcast_to(far_rows[None], (SIDE * NEAR, *far_rows.shape))
    quads = lax.all_to_all(quads, QUAD, 0, 0, tiled=True)
    quads, feature_rows = lax.optimization_barrier((quads, feature_rows))
    panels = quads.reshape(SIDE, NEAR, FAR * MID, own_rows, 3 * hidden_width)
    panels = panels.swapaxes(1, 2).reshape(feature_count, 3 * hidden_width)
    both_panels = panels[:, : 2 * hidden_width]
    down_panel = panels[:, 2 * hidden_width :]

    projected = jnp.dot(tokens, both_panels, preferred_element_type=jnp.float32)
    back = jnp.dot(grad_out, down_panel, preferred_element_type=jnp.float32)
    gate_val = projected[:, :hidden_width]
    up_val = projected[:, hidden_width:]
    hidden_grad = token_gate[:, None] * back
    gate_sigmoid = jax.nn.sigmoid(gate_val)
    grad_up = hidden_grad * (gate_val * gate_sigmoid)
    grad_gate = hidden_grad * up_val * gate_sigmoid * (1.0 + gate_val * (1.0 - gate_sigmoid))
    grads = jnp.concatenate([grad_gate, grad_up], axis=1).astype(jnp.bfloat16)

    turned = jnp.concatenate([grads[half_slots:], grads[:half_slots]], axis=0)
    sent_grads = jnp.where(core_index == 0, grads, turned)
    partner_grads = lax.ppermute(sent_grads, "side", SWAP)

    input_terms = lax.dot_general(
        both_panels, grads, COLS_CONTRACT, preferred_element_type=jnp.float32
    ).astype(jnp.bfloat16)
    own_features = feature_count // (WIDE * RING * CORE)
    by_expert = input_terms.reshape(WIDE, RING, CORE, own_features, slot_count)
    core_sent = part_for(by_expert, "core", 2, 1)
    core_terms = [part_for(by_expert, "core", 2, 0), moved(core_sent, "core", 1)]

    partner_grads, _ = lax.optimization_barrier((partner_grads, core_sent))
    both_grads = jnp.concatenate([grads, partner_grads], axis=0)
    weight_terms = jnp.dot(
        feature_rows.reshape(half_features, SIDE * slot_count),
        both_grads,
        preferred_element_type=jnp.float32,
    ).astype(jnp.bfloat16)
    weight_terms = weight_terms.reshape(MID * NEAR, FAR, own_rows, 2 * hidden_width)
    near_terms = lax.all_to_all(weight_terms, NEIGHBOURS, 0, 0, tiled=True)

    core_sum = summed(core_terms).astype(jnp.bfloat16)
    ring_terms = [part_for(core_sum, "ring", 1, 0)]
    for shift in (1, RING - 1):
        ring_terms.append(moved(part_for(core_sum, "ring", 1, shift), "ring", shift))
    across_sent = part_for(core_sum, "ring", 1, 2)
    near_terms, ring_terms, across_sent = lax.optimization_barrier(
        (near_terms, ring_terms, across_sent)
    )
    near_sum = summed([near_terms[i] for i in range(MID * NEAR)]).astype(jnp.bfloat16)
    weight_share = exchanged_sum(near_sum, "far")

    ring_terms.append(moved(across_sent, "ring", 2))
    ring_sum = summed(ring_terms).astype(jnp.bfloat16)
    wide_terms = [part_for(ring_sum, "wide", 0, 0), moved(part_for(ring_sum, "wide", 0, 1), "wide", 1)]
    grad_tokens = summed(wide_terms).astype(jnp.bfloat16).T
    grad_scale = float(SIDE * FAR * MID * NEAR * slot_count) ** (-0.5)
    weight_share = weight_share * grad_scale
    return grad_tokens, weight_share[:, :hidden_width], weight_share[:, hidden_width:]


def solution(mesh):
    fine_mesh = Mesh(mesh.devices.reshape(tuple(SIZES.values())), tuple(SIZES))
    in_specs = (P(DP, None), P(DP, None), P(DP), P(DP), P(DP)) + (P(DP, EXPERT),) * 3
    out_specs = (P(DP, EXPERT),) * 3
    return jax.shard_map(
        local, mesh=fine_mesh, in_specs=in_specs, out_specs=out_specs, check_vma=False
    )
```

```python
import jax
import jax.numpy as jnp
from jax import lax
from jax.experimental.layout import Layout, with_layout_constraint
from jax.sharding import Mesh, PartitionSpec as P

BLOCK = 128
SIZES = {"side": 2, "far": 8, "mid": 2, "near": 2, "wide": 2, "ring": 4, "core": 2}
SIDE, FAR, MID, NEAR, WIDE, RING, CORE = SIZES.values()
DP = ("side", "far", "mid", "near")
SECONDS = ("far", "mid")
QUAD = ("side", "near")
NEIGHBOURS = ("mid", "near")
SWAP = [(0, 1), (1, 0)]
EXPERT = ("wide", "ring", "core")

ROWS_CONTRACT = (((0,), (0,)), ((), ()))
COLS_CONTRACT = (((1,), (1,)), ((), ()))


def row_major(array):
    return with_layout_constraint(array, Layout(major_to_minor=(0, 1)))


def summed(terms):
    total = terms[0].astype(jnp.float32)
    for term in terms[1:]:
        total = total + term.astype(jnp.float32)
    return total


def part_for(parts, axis, dim, shift):
    index = (lax.axis_index(axis) + shift) % SIZES[axis]
    return lax.dynamic_index_in_dim(parts, index, dim, keepdims=False)


def moved(part, axis, shift):
    return lax.ppermute(part, axis, [(i, (i + shift) % SIZES[axis]) for i in range(SIZES[axis])])


def exchanged_sum(parts, axes):
    terms = lax.all_to_all(parts, axes, 0, 0, tiled=True)
    return summed([terms[i] for i in range(terms.shape[0])])


def local(
    tokens, grad_out, route_rows, route_gate, block_count, gate_weight, up_weight, down_weight_t
):
    own_rows, hidden_width = gate_weight.shape
    slot_count = route_rows.shape[0]
    feature_count = tokens.shape[1]

    slots = jnp.arange(slot_count, dtype=jnp.int32)
    slot_gate = jnp.where(slots // BLOCK < block_count[0], route_gate, 0.0)
    carried = route_rows[:, None] == slots[None, :]
    token_gate = jnp.sum(jnp.where(carried, slot_gate[:, None], 0.0), axis=0)

    side_index = lax.axis_index("side")
    core_index = lax.axis_index("core")
    half_features = feature_count // SIDE
    half_slots = slot_count // CORE
    sent_tokens = lax.dynamic_slice(
        tokens,
        (core_index * half_slots, (1 - side_index) * half_features),
        (half_slots, half_features),
    )
    fetched_tokens = row_major(lax.ppermute(row_major(sent_tokens), "side", SWAP))

    owned = jnp.concatenate([gate_weight, up_weight, down_weight_t], axis=1)
    far_rows = lax.all_gather(owned, SECONDS, axis=0, tiled=True)
    far_rows, fetched_tokens, early_tokens = lax.optimization_barrier(
        (far_rows, fetched_tokens, tokens)
    )
    swapped_tokens = row_major(lax.ppermute(fetched_tokens, "core", SWAP))
    kept_tokens = lax.dynamic_slice_in_dim(early_tokens, side_index * half_features, half_features, 1)
    feature_rows = jnp.concatenate([kept_tokens, fetched_tokens, swapped_tokens], axis=0).T
    feature_rows = feature_rows.reshape(FAR, MID * NEAR, own_rows, SIDE * slot_count)
    feature_rows = lax.optimization_barrier(feature_rows.swapaxes(0, 1))
    quads = jnp.broadcast_to(far_rows[None], (SIDE * NEAR, *far_rows.shape))
    quads = lax.all_to_all(quads, QUAD, 0, 0, tiled=True)
    quads, feature_rows = lax.optimization_barrier((quads, feature_rows))
    panels = quads.reshape(SIDE, NEAR, FAR * MID, own_rows, 3 * hidden_width)
    panels = panels.swapaxes(1, 2).reshape(feature_count, 3 * hidden_width)
    both_panels = panels[:, : 2 * hidden_width]
    down_panel = panels[:, 2 * hidden_width :]

    projected = jnp.dot(tokens, both_panels, preferred_element_type=jnp.float32)
    back = jnp.dot(grad_out, down_panel, preferred_element_type=jnp.float32)
    gate_val = projected[:, :hidden_width]
    up_val = projected[:, hidden_width:]
    hidden_grad = token_gate[:, None] * back
    gate_sigmoid = jax.nn.sigmoid(gate_val)
    grad_up = hidden_grad * (gate_val * gate_sigmoid)
    grad_gate = hidden_grad * up_val * gate_sigmoid * (1.0 + gate_val * (1.0 - gate_sigmoid))
    grads = jnp.concatenate([grad_gate, grad_up], axis=1).astype(jnp.bfloat16)

    turned = jnp.concatenate([grads[half_slots:], grads[:half_slots]], axis=0)
    sent_grads = jnp.where(core_index == 0, grads, turned)
    partner_grads = lax.ppermute(sent_grads, "side", SWAP)

    input_terms = lax.dot_general(
        both_panels, grads, COLS_CONTRACT, preferred_element_type=jnp.float32
    ).astype(jnp.bfloat16)
    own_features = feature_count // (WIDE * RING * CORE)
    by_expert = input_terms.reshape(WIDE, RING, CORE, own_features, slot_count)
    core_sent = part_for(by_expert, "core", 2, 1)
    core_terms = [part_for(by_expert, "core", 2, 0), moved(core_sent, "core", 1)]

    partner_grads, _ = lax.optimization_barrier((partner_grads, core_sent))
    both_grads = jnp.concatenate([grads, partner_grads], axis=0)
    weight_terms = jnp.dot(
        feature_rows.reshape(half_features, SIDE * slot_count),
        both_grads,
        preferred_element_type=jnp.float32,
    ).astype(jnp.bfloat16)
    weight_terms = weight_terms.reshape(MID * NEAR, FAR, own_rows, 2 * hidden_width)
    near_terms = lax.all_to_all(weight_terms, NEIGHBOURS, 0, 0, tiled=True)

    core_sum = summed(core_terms).astype(jnp.bfloat16)
    ring_terms = [
        part_for(core_sum, "ring", 1, 0),
        moved(part_for(core_sum, "ring", 1, 1), "ring", 1),
    ]
    ring_sent = [part_for(core_sum, "ring", 1, shift) for shift in range(2, RING)]
    near_terms, ring_terms, ring_sent = lax.optimization_barrier(
        (near_terms, ring_terms, ring_sent)
    )
    near_sum = summed([near_terms[i] for i in range(MID * NEAR)]).astype(jnp.bfloat16)
    weight_share = exchanged_sum(near_sum, "far")

    ring_terms += [moved(sent, "ring", shift) for shift, sent in enumerate(ring_sent, start=2)]
    ring_sum = summed(ring_terms).astype(jnp.bfloat16)
    wide_terms = [part_for(ring_sum, "wide", 0, 0), moved(part_for(ring_sum, "wide", 0, 1), "wide", 1)]
    grad_tokens = summed(wide_terms).astype(jnp.bfloat16).T
    grad_scale = float(SIDE * FAR * MID * NEAR * slot_count) ** (-0.5)
    weight_share = weight_share * grad_scale
    return grad_tokens, weight_share[:, :hidden_width], weight_share[:, hidden_width:]


def solution(mesh):
    fine_mesh = Mesh(mesh.devices.reshape(tuple(SIZES.values())), tuple(SIZES))
    in_specs = (P(DP, None), P(DP, None), P(DP), P(DP), P(DP)) + (P(DP, EXPERT),) * 3
    out_specs = (P(DP, EXPERT),) * 3
    return jax.shard_map(
        local, mesh=fine_mesh, in_specs=in_specs, out_specs=out_specs, check_vma=False
    )
```

```python
import jax
import jax.numpy as jnp
from jax import lax
from jax.experimental.layout import Layout, with_layout_constraint
from jax.sharding import Mesh, PartitionSpec as P

BLOCK = 128
SIZES = {"side": 2, "far": 8, "mid": 2, "near": 2, "wide": 2, "ring": 4, "core": 2}
SIDE, FAR, MID, NEAR, WIDE, RING, CORE = SIZES.values()
DP = ("side", "far", "mid", "near")
SECONDS = ("far", "mid")
QUAD = ("side", "near")
NEIGHBOURS = ("mid", "near")
SWAP = [(0, 1), (1, 0)]
EXPERT = ("wide", "ring", "core")

ROWS_CONTRACT = (((0,), (0,)), ((), ()))
COLS_CONTRACT = (((1,), (1,)), ((), ()))


def row_major(array):
    return with_layout_constraint(array, Layout(major_to_minor=(0, 1)))


def summed(terms):
    total = terms[0].astype(jnp.float32)
    for term in terms[1:]:
        total = total + term.astype(jnp.float32)
    return total


def part_for(parts, axis, dim, shift):
    index = (lax.axis_index(axis) + shift) % SIZES[axis]
    return lax.dynamic_index_in_dim(parts, index, dim, keepdims=False)


def moved(part, axis, shift):
    return lax.ppermute(part, axis, [(i, (i + shift) % SIZES[axis]) for i in range(SIZES[axis])])


def exchanged_sum(parts, axes):
    terms = lax.all_to_all(parts, axes, 0, 0, tiled=True)
    return summed([terms[i] for i in range(terms.shape[0])])


def local(
    tokens, grad_out, route_rows, route_gate, block_count, gate_weight, up_weight, down_weight_t
):
    own_rows, hidden_width = gate_weight.shape
    slot_count = route_rows.shape[0]
    feature_count = tokens.shape[1]

    slots = jnp.arange(slot_count, dtype=jnp.int32)
    slot_gate = jnp.where(slots // BLOCK < block_count[0], route_gate, 0.0)
    carried = route_rows[:, None] == slots[None, :]
    token_gate = jnp.sum(jnp.where(carried, slot_gate[:, None], 0.0), axis=0)

    side_index = lax.axis_index("side")
    core_index = lax.axis_index("core")
    half_features = feature_count // SIDE
    half_slots = slot_count // CORE
    sent_tokens = lax.dynamic_slice(
        tokens,
        (core_index * half_slots, (1 - side_index) * half_features),
        (half_slots, half_features),
    )
    fetched_tokens = row_major(lax.ppermute(row_major(sent_tokens), "side", SWAP))

    owned = jnp.concatenate([gate_weight, up_weight, down_weight_t], axis=1)
    far_rows = lax.all_gather(owned, SECONDS, axis=0, tiled=True)
    far_rows, fetched_tokens, early_tokens = lax.optimization_barrier(
        (far_rows, fetched_tokens, tokens)
    )
    swapped_tokens = row_major(lax.ppermute(fetched_tokens, "core", SWAP))
    kept_tokens = row_major(
        lax.dynamic_slice_in_dim(early_tokens, side_index * half_features, half_features, 1)
    )
    feature_rows = jnp.concatenate([kept_tokens, fetched_tokens, swapped_tokens], axis=0).T
    feature_rows = feature_rows.reshape(FAR, MID * NEAR, own_rows, SIDE * slot_count)
    feature_rows = lax.optimization_barrier(feature_rows.swapaxes(0, 1))
    near_index = lax.axis_index("near")
    panels = jnp.zeros((SIDE, FAR * MID, NEAR, own_rows, 3 * hidden_width), jnp.bfloat16)
    for side_step, near_step, rows in (
        (0, 0, far_rows),
        (0, 1, lax.ppermute(far_rows, "near", SWAP)),
        (1, 0, lax.ppermute(far_rows, "side", SWAP)),
        (1, 1, lax.ppermute(far_rows, QUAD, [(i, 3 - i) for i in range(4)])),
    ):
        block = rows.reshape(1, FAR * MID, 1, own_rows, 3 * hidden_width)
        place = ((side_index + side_step) % SIDE, 0, (near_index + near_step) % NEAR, 0, 0)
        panels = lax.dynamic_update_slice(panels, block, place)
        if side_step == near_step == 0:
            panels, feature_rows = lax.optimization_barrier((panels, feature_rows))
    panels = panels.reshape(feature_count, 3 * hidden_width)
    both_panels = panels[:, : 2 * hidden_width]
    down_panel = panels[:, 2 * hidden_width :]

    projected = jnp.dot(tokens, both_panels, preferred_element_type=jnp.float32)
    back = jnp.dot(grad_out, down_panel, preferred_element_type=jnp.float32)
    gate_val = projected[:, :hidden_width]
    up_val = projected[:, hidden_width:]
    hidden_grad = token_gate[:, None] * back
    gate_sigmoid = jax.nn.sigmoid(gate_val)
    grad_up = hidden_grad * (gate_val * gate_sigmoid)
    grad_gate = hidden_grad * up_val * gate_sigmoid * (1.0 + gate_val * (1.0 - gate_sigmoid))
    grads = jnp.concatenate([grad_gate, grad_up], axis=1).astype(jnp.bfloat16)

    turned = jnp.concatenate([grads[half_slots:], grads[:half_slots]], axis=0)
    sent_grads = jnp.where(core_index == 0, grads, turned)
    partner_grads = lax.ppermute(sent_grads, "side", SWAP)

    input_terms = lax.dot_general(
        both_panels, grads, COLS_CONTRACT, preferred_element_type=jnp.float32
    ).astype(jnp.bfloat16)
    own_features = feature_count // (WIDE * RING * CORE)
    by_expert = input_terms.reshape(WIDE, RING, CORE, own_features, slot_count)
    core_sent = part_for(by_expert, "core", 2, 1)
    core_terms = [part_for(by_expert, "core", 2, 0), moved(core_sent, "core", 1)]

    partner_grads, _ = lax.optimization_barrier((partner_grads, core_sent))
    both_grads = jnp.concatenate([grads, partner_grads], axis=0)
    weight_terms = jnp.dot(
        feature_rows.reshape(half_features, SIDE * slot_count),
        both_grads,
        preferred_element_type=jnp.float32,
    ).astype(jnp.bfloat16)
    weight_terms = weight_terms.reshape(MID * NEAR, FAR, own_rows, 2 * hidden_width)
    near_terms = lax.all_to_all(weight_terms, NEIGHBOURS, 0, 0, tiled=True)

    core_sum = summed(core_terms).astype(jnp.bfloat16)
    ring_terms = [
        part_for(core_sum, "ring", 1, 0),
        moved(part_for(core_sum, "ring", 1, 1), "ring", 1),
    ]
    ring_sent = [part_for(core_sum, "ring", 1, shift) for shift in range(2, RING)]
    near_terms, ring_terms, ring_sent = lax.optimization_barrier(
        (near_terms, ring_terms, ring_sent)
    )
    near_sum = summed([near_terms[i] for i in range(MID * NEAR)]).astype(jnp.bfloat16)
    weight_share = exchanged_sum(near_sum, "far")

    ring_terms += [moved(sent, "ring", shift) for shift, sent in enumerate(ring_sent, start=2)]
    ring_sum = summed(ring_terms).astype(jnp.bfloat16)
    wide_terms = [part_for(ring_sum, "wide", 0, 0), moved(part_for(ring_sum, "wide", 0, 1), "wide", 1)]
    grad_tokens = summed(wide_terms).astype(jnp.bfloat16).T
    grad_scale = float(SIDE * FAR * MID * NEAR * slot_count) ** (-0.5)
    weight_share = weight_share * grad_scale
    return grad_tokens, weight_share[:, :hidden_width], weight_share[:, hidden_width:]


def solution(mesh):
    fine_mesh = Mesh(mesh.devices.reshape(tuple(SIZES.values())), tuple(SIZES))
    in_specs = (P(DP, None), P(DP, None), P(DP), P(DP), P(DP)) + (P(DP, EXPERT),) * 3
    out_specs = (P(DP, EXPERT),) * 3
    return jax.shard_map(
        local, mesh=fine_mesh, in_specs=in_specs, out_specs=out_specs, check_vma=False
    )
```
